32 devices in a mesh: groups: 2 (over x), sector: 16 (over z, y, core).
Axes of the slice: x: 2, y: 2, z: 4, core: 2. Of those that a mesh axis runs over, the one named last changes fastest.
Arguments:
- fields: bfloat16 [524288, 128], P(('groups', 'sector')), parts along dimension 0, may hold values from -6 to 6
- weights: bfloat16 [5120, 128, 128], P('sector'), may hold values from -0.25 to 0.25
- source_block: int32 [5120], P('sector'), may hold values from 0 to 127
- target_block: int32 [1280], P('sector'), may hold values from 0 to 1023, as said below
- area: float32 [131072], P('sector'), may hold values from 0.1 to 1
Outputs:
- level10: bfloat16 [262144, 128], P(('groups', 'sector')), parts along dimension 0
- level9: float32 [65536, 128], P(('groups', 'sector')), parts along dimension 0
- level8: float32 [16384, 128], P(('groups', 'sector')), parts along dimension 0
The draws below stay inside these ranges and needn't reach their ends.
There are 2 independent parts, one for each index of `groups`. The reference program is written for one: setup_inputs(seed, part) draws one part's arguments, and reference() takes and returns one part's arrays. A program takes and returns all parts, laid end to end along the dimension named above; an argument that names none is the same for every part. Nothing has to cross between parts.
Inputs may be any that keep to these rules, and one draw needn't show every extreme that they name: `target_block`: the partial blocks of one sector s (indices s * 80 to s * 80 + 79) name distinct target blocks; each target block b lies in sector b // 64, at most 2 sectors from s around the closed loop; at most 16 of them lie in any one sector other than s, and every sector has exactly 16 in one other sector.
All inputs are finite; a program needn't handle non-finite values.
Results may differ from the reference program's by a relative error of at most 0.0075.
Values may be sent and summed in bfloat16 or wider, within the bound.
A program may use at most 128 MiB of HBM per device.

```python
import math
import jax
import jax.numpy as jnp
from jax import lax

BLK = 128
PER_TGT = 4
REACH = 2
TB_DEV = 64
CAP = 16
NG_DEV = 80
SB_DEV = 128
NB_DEV = 320
COLS = 128
NPIX = 131072
NSRC = 262144
N_SECTOR = 16


def draw_target_block(key, part):
    width = 2 * REACH
    key_counts, key_forced, key_perms, key_order = jax.random.split(key, 4)
    others = jax.random.randint(key_counts, (N_SECTOR, width), 1, CAP + 1)
    forced = jax.random.randint(key_forced, (N_SECTOR,), 0, width)
    others = jnp.where(jnp.arange(width)[None, :] == forced[:, None], CAP, others)
    middle = NG_DEV - jnp.sum(others, axis=1)
    counts = jnp.concatenate([others[:, :REACH], middle[:, None], others[:, REACH:]], axis=1)
    ends = jnp.cumsum(counts, axis=1)
    starts = ends - counts
    slots = jnp.arange(NG_DEV)
    which = jnp.sum(slots[None, :, None] >= ends[:, None, :], axis=2)
    within = slots[None, :] - jnp.take_along_axis(starts, which, axis=1)
    perm_keys = jax.random.split(key_perms, N_SECTOR * (width + 1))
    perms = jax.vmap(lambda single: jax.random.permutation(single, TB_DEV))(perm_keys)
    perms = perms.reshape(N_SECTOR, width + 1, TB_DEV)
    chosen = perms[jnp.arange(N_SECTOR)[:, None], which, within]
    owners = (jnp.arange(N_SECTOR)[:, None] + which - REACH) % N_SECTOR
    blocks = owners * TB_DEV + chosen
    order_keys = jax.random.split(key_order, N_SECTOR)
    orders = jax.vmap(lambda single: jax.random.permutation(single, NG_DEV))(order_keys)
    blocks = jnp.take_along_axis(blocks, orders, axis=1)
    return blocks.reshape(-1).astype(jnp.int32)


def with_ends(array, own_key, least, high):
    longest = array.shape.index(max(array.shape))
    spots = []
    for shift in (0, 1):
        where = [jax.random.randint(jax.random.fold_in(own_key, axis), (), 0, length) for axis, length in enumerate(array.shape)]
        where[longest] = (where[longest] + shift) % array.shape[longest]
        spots.append(tuple(where))
    return array.at[spots[0]].set(least).at[spots[1]].set(high)


def block_levels(rng, extent, cuts, least, largest):
    level, own = 1.0, jax.random.fold_in(rng, 6)
    for dim, shards_of in cuts:
        steps = jnp.exp(jax.random.uniform(jax.random.fold_in(own, dim), (shards_of,), jnp.float32, least / len(cuts), largest / len(cuts)))
        level = level * jnp.repeat(steps, extent[dim] // shards_of).reshape([-1 if axis == dim else 1 for axis in range(len(extent))])
    return level


def gaussian(rng, shape, scale, limit, cuts=(), kind=jnp.bfloat16):
    entries = jax.random.normal(rng, shape, jnp.float32) * scale
    if len(cuts) > 0:
        entries = block_levels(rng, shape, cuts, -0.22, 0.18) * entries
    return jnp.clip(entries, min=-limit, max=limit).astype(kind)


def setup_inputs(seed: int = 0, part: int = 0) -> dict:
    seeds = jax.random.split(jax.random.key(seed), 6)
    part_keys = jax.random.split(jax.random.fold_in(seeds[5], part), 6)
    fields = gaussian(part_keys[0], (NSRC, COLS), 1.0, 6.0, ((0, 16),))
    weights = gaussian(seeds[1], (NB_DEV * N_SECTOR, BLK, BLK), (BLK * PER_TGT) ** -0.5, 0.25, ((0, 16),))
    source_block = with_ends(jax.random.randint(seeds[2], (NB_DEV * N_SECTOR,), 0, SB_DEV), jax.random.fold_in(seeds[2], 1), 0, SB_DEV - 1).astype(jnp.int32)
    target_block = draw_target_block(jax.random.fold_in(seeds[5], 71), part)
    area = jnp.clip(jnp.exp(math.log(1.0) - 2.3025851 * jax.random.uniform(seeds[4], (NPIX,), jnp.float32) ** block_levels(seeds[4], (NPIX,), ((0, 16),), -0.2, 0.2)), 0.1, 1.0)
    return dict(fields=fields, weights=weights, source_block=source_block, target_block=target_block, area=area)


def reference(fields, weights, source_block, target_block, area):
    cols = fields.shape[1]
    source_blocks = fields.reshape(-1, BLK, cols)
    weight_dev = weights.reshape(N_SECTOR, NB_DEV, BLK, BLK)
    source_dev = source_block.reshape(N_SECTOR, NB_DEV)
    target_dev = target_block.reshape(N_SECTOR, NG_DEV)
    sector_ids = jnp.arange(N_SECTOR).astype(jnp.int32)

    def one_sector(summed, items):
        wblocks, sources, targets, sector_id = items
        start = (sector_id * SB_DEV).astype(jnp.int32)
        own_blocks = lax.dynamic_slice_in_dim(source_blocks, start, SB_DEV, 0)
        picked = own_blocks[sources.astype(jnp.int32)]
        terms = jnp.einsum("kps,ksc->kpc", wblocks.astype(jnp.float32), picked.astype(jnp.float32))
        partial_value = terms.reshape(NG_DEV, PER_TGT, BLK, cols).sum(1).astype(jnp.bfloat16)
        summed = summed.at[targets.astype(jnp.int32)].add(partial_value.astype(jnp.float32))
        return summed, None

    start_sum = jnp.zeros((TB_DEV * N_SECTOR, BLK, cols), jnp.float32)
    summed, unused = lax.scan(one_sector, start_sum, (weight_dev, source_dev, target_dev, sector_ids))
    flat = summed.reshape(-1, cols)
    level10 = flat.astype(jnp.bfloat16)
    weighted = flat * area[:, None]
    level9 = weighted.reshape(-1, 4, cols).sum(1) / area.reshape(-1, 4).sum(1)[:, None]
    level8 = weighted.reshape(-1, 16, cols).sum(1) / area.reshape(-1, 16).sum(1)[:, None]
    return level10, level9, level8
```

```python
import functools

import jax
import jax.numpy as jnp
from jax import lax
from jax.experimental import pallas as pl
from jax.experimental.pallas import tpu as pltpu
from jax.sharding import PartitionSpec as P

CAP = 16
MOVES = (2, -2, 1, -1)
CHUNK = 8


def shifted(block, axis, distance):
    size = lax.axis_size(axis)
    route = [((i - distance) % size, i) for i in range(size)]
    return lax.ppermute(block, axis, route)


def remap_kernel(
    sectors, owned, per_group, source, target, w_hbm, f_hbm, *rest
):
    sends = rest[:4]
    own_out, wbuf, fbuf, obuf, count, w_sem, f_sem, o_sem = rest[4:]
    groups_dev = target.shape[0]
    chunks = groups_dev // CHUNK
    per_chunk = CHUNK * per_group
    f_copy = pltpu.make_async_copy(f_hbm, fbuf, f_sem)
    f_copy.start()

    def w_copy(c):
        rows = pl.ds(c * per_chunk, per_chunk)
        return pltpu.make_async_copy(w_hbm.at[rows], wbuf.at[rows], w_sem.at[c])

    for c in range(chunks):
        w_copy(c).start()
    me = lax.axis_index("sector")
    for k in range(4):
        count[k] = 0

    @pl.loop(0, owned)
    def _(t):
        obuf[t] = jnp.zeros(obuf.shape[1:], obuf.dtype)

    f_copy.wait()

    @pl.loop(0, chunks)
    def _(c):
        w_copy(c).wait()
        for p in range(CHUNK):
            g = c * CHUNK + p
            first = g * per_group
            left = jnp.concatenate([wbuf[first + q] for q in range(per_group)], axis=1)
            right = jnp.concatenate(
                [fbuf[source[first + q]] for q in range(per_group)], axis=0
            )
            value = jnp.dot(left, right, preferred_element_type=jnp.float32)
            where_to = target[g]
            distance = lax.rem(where_to // owned - me + sectors, sectors)
            mine = distance == 0
            kind = jnp.where(
                distance == 2, 0, jnp.where(distance == 1, 2, jnp.where(distance == sectors - 1, 3, 1))
            )
            rank = count[kind]
            count[kind] = rank + jnp.where(mine, 0, 1)
            slot = jnp.where(mine, lax.rem(where_to, owned), owned + CAP * kind + rank)
            obuf[slot] = value.astype(obuf.dtype)

    copies = [
        pltpu.make_async_copy(obuf.at[pl.ds(owned + CAP * k, CAP)], sends[k], o_sem.at[k])
        for k in range(4)
    ]
    copies.append(pltpu.make_async_copy(obuf.at[pl.ds(0, owned)], own_out, o_sem.at[4]))
    for copy in copies:
        copy.start()
    for copy in copies:
        copy.wait()


def remap(fields, weights, source_block, target_block, owned, sectors):
    nb, width, _ = weights.shape
    cols = fields.shape[-1]
    groups_dev = target_block.shape[0]
    block = (width, cols)
    hbm = pl.BlockSpec(memory_space=pl.ANY)
    smem = pl.BlockSpec(memory_space=pltpu.SMEM)
    return pl.pallas_call(
        functools.partial(remap_kernel, sectors, owned, nb // groups_dev),
        out_shape=[jax.ShapeDtypeStruct((CAP, *block), jnp.bfloat16)] * 4
        + [jax.ShapeDtypeStruct((owned, *block), jnp.bfloat16)],
        in_specs=[smem, smem, hbm, hbm],
        out_specs=[hbm] * 5,
        scratch_shapes=[
            pltpu.VMEM(weights.shape, jnp.bfloat16),
            pltpu.VMEM(fields.shape, jnp.bfloat16),
            pltpu.VMEM((owned + 4 * CAP, *block), jnp.bfloat16),
            pltpu.SMEM((4,), jnp.int32),
            pltpu.SemaphoreType.DMA((groups_dev // CHUNK,)),
            pltpu.SemaphoreType.DMA,
            pltpu.SemaphoreType.DMA((5,)),
        ],
        compiler_params=pltpu.CompilerParams(vmem_limit_bytes=40 * 2**20),
        cost_estimate=pl.CostEstimate(
            flops=2 * nb * width * width * cols, bytes_accessed=19 * 2**20, transcendentals=0
        ),
        name="remap",
    )(source_block, target_block, weights, fields)


STEP = 8


def combine_kernel(slots, own, r0, r1, r2, r3, pool, ten, nine, eight):
    base = pl.program_id(0) * STEP
    received = (r0, r1, r2, r3)
    n9 = nine.shape[1]
    for j in range(STEP):
        total = own[j].astype(jnp.float32)
        for k in range(4):
            slot = slots[k, base + j]
            part = received[k][jnp.maximum(slot, 0)].astype(jnp.float32)
            total = total + jnp.where(slot >= 0, part, 0.0)
        rounded = total.astype(jnp.bfloat16)
        ten[j] = rounded
        means = jnp.dot(pool[j], rounded, preferred_element_type=jnp.float32)
        nine[j] = means[:n9]
        eight[j] = means[n9:]


def combine(slots, own, received, pool):
    owned, width, cols = own.shape
    n9, n8 = width // 4, width // 16
    whole = pl.BlockSpec(memory_space=pltpu.VMEM)

    def rows(n):
        return pl.BlockSpec((STEP, n, cols), lambda i: (i, 0, 0))

    return pl.pallas_call(
        combine_kernel,
        grid=(owned // STEP,),
        out_shape=[
            jax.ShapeDtypeStruct((owned, width, cols), jnp.bfloat16),
            jax.ShapeDtypeStruct((owned, n9, cols), jnp.float32),
            jax.ShapeDtypeStruct((owned, n8, cols), jnp.float32),
        ],
        in_specs=[pl.BlockSpec(memory_space=pltpu.SMEM), rows(width)]
        + [whole] * 4
        + [pl.BlockSpec((STEP, n9 + n8, width), lambda i: (i, 0, 0))],
        out_specs=[rows(width), rows(n9), rows(n8)],
        compiler_params=pltpu.CompilerParams(vmem_limit_bytes=24 * 2**20),
        cost_estimate=pl.CostEstimate(
            flops=2 * owned * 40 * width * cols, bytes_accessed=8 * 2**20, transcendentals=0
        ),
        name="combine",
    )(slots, own, *received, pool)


def pool_matrix(area, width):
    rows = area.reshape(-1, 1, width)
    pixel = jnp.arange(width)
    member = jnp.concatenate(
        [
            pixel[None, :] // 4 == jnp.arange(width // 4)[:, None],
            pixel[None, :] // 16 == jnp.arange(width // 16)[:, None],
        ],
        axis=0,
    )
    chosen = jnp.where(member[None], rows, 0.0)
    return (chosen / chosen.sum(2, keepdims=True)).astype(jnp.bfloat16)


def receive_slots(targets, me, owned):
    mine = targets // owned == me
    rank = jnp.cumsum(mine.astype(jnp.int32), axis=1)
    here = targets[:, None, :] == me * owned + jnp.arange(owned)[None, :, None]
    return jnp.sum(jnp.where(here, rank[:, None, :], 0), axis=2) - 1


def per_device(fields, weights, source_block, target_block, area):
    width = weights.shape[1]
    cols = fields.shape[1]
    owned = area.shape[0] // width
    sectors = lax.axis_size("sector")
    me = lax.axis_index("sector")
    targets = jnp.stack([shifted(target_block, "sector", move) for move in MOVES])
    outs = remap(
        fields.reshape(-1, width, cols), weights, source_block, target_block, owned, sectors
    )
    received = [shifted(outs[k], "sector", move) for k, move in enumerate(MOVES)]
    slots = receive_slots(targets, me, owned)
    pool = pool_matrix(area, width)
    ten, nine, eight = combine(slots, outs[4], received, pool)
    return ten.reshape(-1, cols), nine.reshape(-1, cols), eight.reshape(-1, cols)


def solution(mesh):
    in_specs = (
        P(("groups", "sector"), None),
        P("sector", None, None),
        P("sector"),
        P("sector"),
        P("sector"),
    )
    out_specs = (P(("groups", "sector"), None),) * 3
    return jax.shard_map(
        per_device, mesh=mesh, in_specs=in_specs, out_specs=out_specs, check_vma=False
    )
```

```python
import functools

import jax
import jax.numpy as jnp
from jax import lax
from jax.experimental import pallas as pl
from jax.experimental.pallas import tpu as pltpu
from jax.sharding import PartitionSpec as P

CAP = 16
MOVES = (2, -2, 1, -1)
CHUNK = 8
STEP = 8
HBM = pl.BlockSpec(memory_space=pl.ANY)


def product(wbuf, fbuf, source, w_first, s_first, per_group):
    left = jnp.concatenate([wbuf[w_first + q] for q in range(per_group)], axis=1)
    right = jnp.concatenate(
        [fbuf[source[s_first + q]] for q in range(per_group)], axis=0
    )
    value = jnp.dot(left, right, preferred_element_type=jnp.float32)
    return value.astype(jnp.bfloat16)


def field_copies(f_hbm, fbuf, f_sem, parts):
    rows = fbuf.shape[0] // parts
    return [
        pltpu.make_async_copy(
            f_hbm.at[pl.ds(i * rows, rows)], fbuf.at[pl.ds(i * rows, rows)], f_sem.at[i]
        )
        for i in range(parts)
    ]


def outgoing_kernel(sectors, owned, per_group, source_hbm, target_hbm, w_hbm, f_hbm, *rest):
    sends, tables_out = rest[:4], rest[4:9]
    source, target = rest[9:11]
    tables = rest[11:16]
    wbuf, fbuf, obuf, count, chosen, i_sem, w_sem, f_sem, o_sem = rest[16:]
    groups_dev = target.shape[0]
    index_copies = [
        pltpu.make_async_copy(target_hbm, target, i_sem.at[0]),
        pltpu.make_async_copy(source_hbm, source, i_sem.at[1]),
    ]
    for copy in index_copies:
        copy.start()
    fields_in = field_copies(f_hbm, fbuf, f_sem, f_sem.shape[0])
    for copy in fields_in:
        copy.start()
    me = lax.axis_index("sector")
    for k in range(5):
        count[k] = 0

    @pl.loop(0, owned, unroll=8)
    def _(t):
        for table in tables:
            table[t] = -1

    def w_copy(g, slot):
        return pltpu.make_async_copy(
            w_hbm.at[pl.ds(g * per_group, per_group)],
            wbuf.at[pl.ds(slot * per_group, per_group)],
            w_sem.at[slot],
        )

    for copy in index_copies:
        copy.wait()

    for k, move in enumerate(MOVES):
        owner = lax.rem(me + sectors + move, sectors)
        first = owner * owned

        @pl.loop(0, groups_dev, unroll=4)
        def _(g):
            local = target[g] - first

            @pl.when((local >= 0) & (local < owned))
            def _():
                rank = count[k]
                count[k] = rank + 1
                chosen[k * CAP + rank] = g
                tables[k][local] = rank
                w_copy(g, k * CAP + rank).start()

    @pl.loop(0, groups_dev, unroll=4)
    def _(g):
        local = target[g] - me * owned

        @pl.when((local >= 0) & (local < owned))
        def _():
            tables[4][local] = g

    table_copies = [
        pltpu.make_async_copy(tables[k], tables_out[k], o_sem.at[4 + k]) for k in range(5)
    ]
    for copy in table_copies:
        copy.start()
    for copy in fields_in:
        copy.wait()

    copies = []
    for k in range(4):

        @pl.loop(0, count[k])
        def _(rank):
            slot = k * CAP + rank
            g = chosen[slot]
            w_copy(g, slot).wait()
            obuf[slot] = product(
                wbuf, fbuf, source, slot * per_group, g * per_group, per_group
            )

        copies.append(
            pltpu.make_async_copy(obuf.at[pl.ds(CAP * k, CAP)], sends[k], o_sem.at[k])
        )
        copies[-1].start()
    for copy in copies + table_copies:
        copy.wait()


def outgoing(fields, weights, source_block, target_block, owned, sectors):
    nb, width, _ = weights.shape
    cols = fields.shape[-1]
    groups_dev = target_block.shape[0]
    per_group = nb // groups_dev
    block = (width, cols)
    table = -(-owned // 128) * 128
    return pl.pallas_call(
        functools.partial(outgoing_kernel, sectors, owned, per_group),
        out_shape=[jax.ShapeDtypeStruct((CAP, *block), jnp.bfloat16)] * 4
        + [jax.ShapeDtypeStruct((table,), jnp.int32)] * 5,
        in_specs=[HBM] * 4,
        out_specs=[HBM] * 9,
        scratch_shapes=[pltpu.SMEM((nb,), jnp.int32), pltpu.SMEM((groups_dev,), jnp.int32)]
        + [pltpu.SMEM((table,), jnp.int32)] * 5
        + [
            pltpu.VMEM((4 * CAP * per_group, width, width), jnp.bfloat16),
            pltpu.VMEM(fields.shape, jnp.bfloat16),
            pltpu.VMEM((4 * CAP, *block), jnp.bfloat16),
            pltpu.SMEM((5,), jnp.int32),
            pltpu.SMEM((4 * CAP,), jnp.int32),
            pltpu.SemaphoreType.DMA((2,)),
            pltpu.SemaphoreType.DMA((4 * CAP,)),
            pltpu.SemaphoreType.DMA((4,)),
            pltpu.SemaphoreType.DMA((9,)),
        ],
        compiler_params=pltpu.CompilerParams(vmem_limit_bytes=60 * 2**20),
        name="outgoing",
    )(source_block, target_block, weights, fields)


def exchange_kernel(per_group, sectors, *refs):
    sends, tables = refs[:4], refs[4:8]
    own_table_hbm, source_hbm, w_hbm, f_hbm, area = refs[8:13]
    received, tables_out, own_out, pool = refs[13:17], refs[17:21], refs[21], refs[22]
    own_table, source, wbuf, fbuf, pbuf, obuf = refs[23:29]
    send_sem, recv_sem, i_sem, w_sem, f_sem, o_sem = refs[29:]
    me = lax.axis_index("sector")
    chunks = w_sem.shape[0]
    per_chunk = CHUNK * per_group
    owned = obuf.shape[0]
    barrier = pltpu.get_barrier_semaphore()
    for move in MOVES:
        pl.semaphore_signal(
            barrier,
            inc=1,
            device_id={"sector": lax.rem(me + sectors + move, sectors)},
            device_id_type=pl.DeviceIdType.MESH,
        )
    pl.semaphore_wait(barrier, len(MOVES))
    remote = []
    for k, move in enumerate(MOVES):
        peer = {"sector": lax.rem(me + sectors + move, sectors)}
        for index, source_ref, target_ref in (
            (k, sends[k], received[k]),
            (4 + k, tables[k], tables_out[k]),
        ):
            remote.append(
                pltpu.make_async_remote_copy(
                    src_ref=source_ref,
                    dst_ref=target_ref,
                    send_sem=send_sem.at[index],
                    recv_sem=recv_sem.at[index],
                    device_id=peer,
                    device_id_type=pl.DeviceIdType.MESH,
                )
            )
            remote[-1].start()
    index_copies = [
        pltpu.make_async_copy(own_table_hbm, own_table, i_sem.at[0]),
        pltpu.make_async_copy(source_hbm, source, i_sem.at[1]),
    ]
    local = index_copies + field_copies(f_hbm, fbuf, f_sem, f_sem.shape[0])
    for copy in local:
        copy.start()

    def w_copy(c):
        rows = pl.ds(c * per_chunk, per_chunk)
        return pltpu.make_async_copy(w_hbm.at[rows], wbuf.at[rows], w_sem.at[c])

    for c in range(chunks):
        w_copy(c).start()
    width = area.shape[1]
    rows = pool.shape[1]
    n9 = width // 4
    row = lax.broadcasted_iota(jnp.int32, (rows, width), 0)
    pixel = lax.broadcasted_iota(jnp.int32, (rows, width), 1)
    member = jnp.where(row < n9, pixel // 4 - row, pixel // 16 - (row - n9)) == 0

    @pl.loop(0, owned)
    def _(t):
        share = jnp.where(member, area[pl.ds(t, 1), :], 0.0)
        pool[t] = (share / share.sum(1, keepdims=True)).astype(pool.dtype)

    for copy in local:
        copy.wait()

    @pl.loop(0, chunks)
    def _(c):
        w_copy(c).wait()

        @pl.loop(0, CHUNK)
        def _(p):
            g = c * CHUNK + p
            pbuf[g] = product(wbuf, fbuf, source, g * per_group, g * per_group, per_group)

    @pl.loop(0, owned)
    def _(t):
        g = own_table[t]
        value = pbuf[jnp.maximum(g, 0)]
        obuf[t] = jnp.where(g >= 0, value.astype(jnp.float32), 0.0).astype(obuf.dtype)

    out = pltpu.make_async_copy(obuf, own_out, o_sem)
    out.start()
    out.wait()
    for copy in remote:
        copy.wait()


def exchange(sends, tables, fields, weights, source_block, area, sectors, groups_dev):
    nb, width, _ = weights.shape
    cols = fields.shape[-1]
    owned = area.shape[0]
    block = (width, cols)
    vmem = pl.BlockSpec(memory_space=pltpu.VMEM)
    table = jax.ShapeDtypeStruct(tables[0].shape, jnp.int32)
    return pl.pallas_call(
        functools.partial(exchange_kernel, nb // groups_dev, sectors),
        out_shape=[jax.ShapeDtypeStruct((CAP, *block), jnp.bfloat16)] * 4
        + [table] * 4
        + [
            jax.ShapeDtypeStruct((owned, *block), jnp.bfloat16),
            jax.ShapeDtypeStruct((owned, width // 4 + width // 16, width), jnp.bfloat16),
        ],
        in_specs=[HBM] * 12 + [vmem],
        out_specs=[HBM] * 9 + [vmem],
        scratch_shapes=[
            pltpu.SMEM(tables[4].shape, jnp.int32),
            pltpu.SMEM((nb,), jnp.int32),
            pltpu.VMEM(weights.shape, jnp.bfloat16),
            pltpu.VMEM(fields.shape, jnp.bfloat16),
            pltpu.VMEM((groups_dev, *block), jnp.bfloat16),
            pltpu.VMEM((owned, *block), jnp.bfloat16),
            pltpu.SemaphoreType.DMA((8,)),
            pltpu.SemaphoreType.DMA((8,)),
            pltpu.SemaphoreType.DMA((2,)),
            pltpu.SemaphoreType.DMA((groups_dev // CHUNK,)),
            pltpu.SemaphoreType.DMA((4,)),
            pltpu.SemaphoreType.DMA,
        ],
        compiler_params=pltpu.CompilerParams(
            collective_id=0, has_side_effects=True, vmem_limit_bytes=60 * 2**20
        ),
        name="exchange",
    )(*sends, *tables, source_block, weights, fields, area)


def combine_kernel(t0, t1, t2, t3, own, r0, r1, r2, r3, pool, ten, nine, eight, *scratch):
    slots, sem = scratch[:4], scratch[4]
    received = (r0, r1, r2, r3)

    @pl.when(pl.program_id(0) == 0)
    def _():
        copies = [
            pltpu.make_async_copy(table, slots[k], sem.at[k])
            for k, table in enumerate((t0, t1, t2, t3))
        ]
        for copy in copies:
            copy.start()
        for copy in copies:
            copy.wait()

    base = pl.program_id(0) * STEP
    n9 = nine.shape[1]
    for j in range(STEP):
        total = own[j].astype(jnp.float32)
        for k in range(4):
            slot = slots[k][base + j]
            part = received[k][jnp.maximum(slot, 0)].astype(jnp.float32)
            total = total + jnp.where(slot >= 0, part, 0.0)
        rounded = total.astype(jnp.bfloat16)
        ten[j] = rounded
        means = jnp.dot(pool[j], rounded, preferred_element_type=jnp.float32)
        nine[j] = means[:n9]
        eight[j] = means[n9:]


def combine(tables, own, received, pool):
    owned, width, cols = own.shape
    n9, n8 = width // 4, width // 16
    whole = pl.BlockSpec(memory_space=pltpu.VMEM)

    def rows(n):
        return pl.BlockSpec((STEP, n, cols), lambda i: (i, 0, 0))

    return pl.pallas_call(
        combine_kernel,
        grid=(owned // STEP,),
        out_shape=[
            jax.ShapeDtypeStruct((owned, width, cols), jnp.bfloat16),
            jax.ShapeDtypeStruct((owned, n9, cols), jnp.float32),
            jax.ShapeDtypeStruct((owned, n8, cols), jnp.float32),
        ],
        in_specs=[HBM] * 4
        + [rows(width)]
        + [whole] * 4
        + [pl.BlockSpec((STEP, n9 + n8, width), lambda i: (i, 0, 0))],
        out_specs=[rows(width), rows(n9), rows(n8)],
        scratch_shapes=[pltpu.SMEM(tables[0].shape, jnp.int32)] * 4
        + [pltpu.SemaphoreType.DMA((4,))],
        compiler_params=pltpu.CompilerParams(vmem_limit_bytes=60 * 2**20),
        name="combine",
    )(*tables, own, *received, pool)


def per_device(fields, weights, source_block, target_block, area):
    width = weights.shape[1]
    cols = fields.shape[1]
    owned = area.shape[0] // width
    sectors = lax.axis_size("sector")
    groups_dev = target_block.shape[0]
    blocks = fields.reshape(-1, width, cols)
    sent = outgoing(blocks, weights, source_block, target_block, owned, sectors)
    arrived = exchange(
        sent[:4], sent[4:], blocks, weights, source_block, area.reshape(owned, width), sectors,
        groups_dev,
    )
    ten, nine, eight = combine(arrived[4:8], arrived[8], arrived[:4], arrived[9])
    return ten.reshape(-1, cols), nine.reshape(-1, cols), eight.reshape(-1, cols)


def solution(mesh):
    in_specs = (
        P(("groups", "sector"), None),
        P("sector", None, None),
        P("sector"),
        P("sector"),
        P("sector"),
    )
    out_specs = (P(("groups", "sector"), None),) * 3
    return jax.shard_map(
        per_device, mesh=mesh, in_specs=in_specs, out_specs=out_specs, check_vma=False
    )
```

```python
import functools

import jax
import jax.numpy as jnp
from jax import lax
from jax.experimental import pallas as pl
from jax.experimental.pallas import tpu as pltpu
from jax.sharding import PartitionSpec as P

CAP = 16
MOVES = (2, -2, 1, -1)
CHUNK = 8
STEP = 8
FIRST = 2
LANES = 128
HBM = pl.BlockSpec(memory_space=pl.ANY)


def product(wbuf, fbuf, source, w_first, s_first, per_group):
    left = jnp.concatenate([wbuf[w_first + q] for q in range(per_group)], axis=1)
    right = jnp.concatenate(
        [fbuf[source[s_first + q]] for q in range(per_group)], axis=0
    )
    value = jnp.dot(left, right, preferred_element_type=jnp.float32)
    return value.astype(jnp.bfloat16)


def field_copies(f_hbm, fbuf, f_sem, parts):
    rows = fbuf.shape[0] // parts
    return [
        pltpu.make_async_copy(
            f_hbm.at[pl.ds(i * rows, rows)], fbuf.at[pl.ds(i * rows, rows)], f_sem.at[i]
        )
        for i in range(parts)
    ]


def table_size(owned):
    width = -(-owned // LANES) * LANES
    return width, (len(MOVES) + 1) * width, -(-(len(MOVES) * CAP + 1) // LANES) * LANES


def outgoing_kernel(sectors, owned, per_group, source_hbm, target_hbm, w_hbm, f_hbm, *rest):
    sends, table_out = rest[:FIRST], rest[FIRST]
    source, target, table, wbuf, fbuf, obuf, count, i_sem, w_sem, f_sem, o_sem = rest[FIRST + 1 :]
    groups_dev = target.shape[0]
    kinds = len(MOVES)
    width, chosen, _ = table_size(owned)
    index_copies = [
        pltpu.make_async_copy(target_hbm, target, i_sem.at[0]),
        pltpu.make_async_copy(source_hbm, source, i_sem.at[1]),
    ]
    for copy in index_copies:
        copy.start()
    fields_in = field_copies(f_hbm, fbuf, f_sem, f_sem.shape[0])
    for copy in fields_in:
        copy.start()
    me = lax.axis_index("sector")
    for k in range(kinds + 1):
        count[k] = 0

    @pl.loop(0, owned, unroll=8)
    def _(t):
        for k in range(kinds + 1):
            table[k * width + t] = -1

    @pl.loop(0, kinds * CAP, unroll=8)
    def _(t):
        table[chosen + t] = 0

    def w_copy(g, slot):
        return pltpu.make_async_copy(
            w_hbm.at[pl.ds(g * per_group, per_group)],
            wbuf.at[pl.ds(slot * per_group, per_group)],
            w_sem.at[slot],
        )

    for copy in index_copies:
        copy.wait()

    @pl.loop(0, groups_dev, unroll=4)
    def _(g):
        where_to = target[g]
        owner = where_to // owned
        local = where_to - owner * owned
        distance = owner - me
        distance = jnp.where(distance < 0, distance + sectors, distance)
        kind = kinds
        for k, move in enumerate(MOVES):
            kind = jnp.where(distance == move % sectors, k, kind)
        rank = count[kind]
        count[kind] = rank + 1
        mine = kind == kinds
        slot = kind * CAP + jnp.where(mine, 0, rank)
        table[chosen + slot] = g
        table[kind * width + local] = jnp.where(mine, g, rank)

        @pl.when(kind < FIRST)
        def _():
            w_copy(g, slot).start()

    table_copy = pltpu.make_async_copy(table, table_out, o_sem.at[FIRST])
    table_copy.start()
    for copy in fields_in:
        copy.wait()

    unroll = 4
    copies = [table_copy]
    for k in range(FIRST):

        @pl.loop(0, (count[k] + unroll - 1) // unroll)
        def _(step):
            for r in range(unroll):
                rank = step * unroll + r
                slot = k * CAP + rank

                @pl.when(rank < count[k])
                def _():
                    w_copy(table[chosen + slot], slot).wait()

            for r in range(unroll):
                slot = k * CAP + step * unroll + r
                g = table[chosen + slot]
                obuf[slot] = product(
                    wbuf, fbuf, source, slot * per_group, g * per_group, per_group
                )

        copy = pltpu.make_async_copy(obuf.at[pl.ds(CAP * k, CAP)], sends[k], o_sem.at[k])
        copy.start()
        copies.append(copy)
    for copy in copies:
        copy.wait()


def outgoing(fields, weights, source_block, target_block, owned, sectors):
    nb, width, _ = weights.shape
    cols = fields.shape[-1]
    groups_dev = target_block.shape[0]
    per_group = nb // groups_dev
    block = (width, cols)
    _, chosen, tail = table_size(owned)
    return pl.pallas_call(
        functools.partial(outgoing_kernel, sectors, owned, per_group),
        out_shape=[jax.ShapeDtypeStruct((CAP, *block), jnp.bfloat16)] * FIRST
        + [jax.ShapeDtypeStruct((chosen + tail,), jnp.int32)],
        in_specs=[HBM] * 4,
        out_specs=[HBM] * (FIRST + 1),
        scratch_shapes=[
            pltpu.SMEM((nb,), jnp.int32),
            pltpu.SMEM((groups_dev,), jnp.int32),
            pltpu.SMEM((chosen + tail,), jnp.int32),
            pltpu.VMEM((FIRST * CAP * per_group, width, width), jnp.bfloat16),
            pltpu.VMEM(fields.shape, jnp.bfloat16),
            pltpu.VMEM((FIRST * CAP, *block), jnp.bfloat16),
            pltpu.SMEM((len(MOVES) + 1,), jnp.int32),
            pltpu.SemaphoreType.DMA((2,)),
            pltpu.SemaphoreType.DMA((FIRST * CAP,)),
            pltpu.SemaphoreType.DMA((4,)),
            pltpu.SemaphoreType.DMA((FIRST + 1,)),
        ],
        compiler_params=pltpu.CompilerParams(vmem_limit_bytes=60 * 2**20),
        name="outgoing",
    )(source_block, target_block, weights, fields)


def exchange_kernel(per_group, sectors, *refs):
    sends, table_hbm = refs[:FIRST], refs[FIRST]
    source_hbm, w_hbm, f_hbm, area = refs[FIRST + 1 : FIRST + 5]
    rest = refs[FIRST + 5 :]
    received, tables_out, own_out, pool = rest[:4], rest[4:8], rest[8], rest[9]
    table, source, wbuf, fbuf, pbuf, obuf, near0, near1 = rest[10:18]
    send_sem, recv_sem, i_sem, w_sem, f_sem, o_sem = rest[18:]
    near = (near0, near1)
    me = lax.axis_index("sector")
    kinds = len(MOVES)
    chunks = w_sem.shape[0]
    per_chunk = CHUNK * per_group
    owned = obuf.shape[0]
    own_row, chosen, _ = table_size(owned)
    own_row = kinds * own_row
    local = [
        pltpu.make_async_copy(table_hbm, table, i_sem.at[0]),
        pltpu.make_async_copy(source_hbm, source, i_sem.at[1]),
    ] + field_copies(f_hbm, fbuf, f_sem, f_sem.shape[0])
    peers = [{"sector": lax.rem(me + sectors + move, sectors)} for move in MOVES]
    barrier = pltpu.get_barrier_semaphore()
    for peer in peers:
        pl.semaphore_signal(
            barrier, inc=1, device_id=peer, device_id_type=pl.DeviceIdType.MESH
        )
    for copy in local:
        copy.start()

    def w_copy(c):
        rows = pl.ds(c * per_chunk, per_chunk)
        return pltpu.make_async_copy(w_hbm.at[rows], wbuf.at[rows], w_sem.at[c])

    pl.semaphore_wait(barrier, kinds)

    def remote(index, k, source_ref, target_ref):
        return pltpu.make_async_remote_copy(
            src_ref=source_ref,
            dst_ref=target_ref,
            send_sem=send_sem.at[index],
            recv_sem=recv_sem.at[index],
            device_id=peers[k],
            device_id_type=pl.DeviceIdType.MESH,
        )

    moved = [remote(k, k, sends[k], received[k]) for k in range(FIRST)]
    moved += [remote(kinds + k, k, table_hbm, tables_out[k]) for k in range(kinds)]
    for copy in moved:
        copy.start()
    for c in range(chunks):
        w_copy(c).start()
    for copy in local:
        copy.wait()

    @pl.loop(0, chunks)
    def _(c):
        w_copy(c).wait()

        @pl.loop(0, CHUNK // 4)
        def _(step):
            for p in range(4):
                g = c * CHUNK + step * 4 + p
                pbuf[g] = product(wbuf, fbuf, source, g * per_group, g * per_group, per_group)

    for k in range(FIRST, kinds):

        @pl.loop(0, CAP)
        def _(rank):
            near[k - FIRST][rank] = pbuf[table[chosen + k * CAP + rank]]

        moved.append(remote(k, k, near[k - FIRST], received[k]))
        moved[-1].start()

    @pl.loop(0, owned)
    def _(t):
        g = table[own_row + t]
        value = pbuf[jnp.maximum(g, 0)]
        obuf[t] = jnp.where(g >= 0, value.astype(jnp.float32), 0.0).astype(obuf.dtype)

    out = pltpu.make_async_copy(obuf, own_out, o_sem)
    out.start()
    width = area.shape[1]
    rows = pool.shape[1]
    n9 = width // 4
    row = lax.broadcasted_iota(jnp.int32, (rows, width), 0)
    pixel = lax.broadcasted_iota(jnp.int32, (rows, width), 1)
    member = jnp.where(row < n9, pixel // 4 - row, pixel // 16 - (row - n9)) == 0

    @pl.loop(0, owned)
    def _(t):
        share = jnp.where(member, area[pl.ds(t, 1), :], 0.0)
        pool[t] = (share / share.sum(1, keepdims=True)).astype(pool.dtype)

    out.wait()
    for copy in moved:
        copy.wait()


def exchange(sends, table, fields, weights, source_block, area, sectors, groups_dev):
    nb, width, _ = weights.shape
    cols = fields.shape[-1]
    owned = area.shape[0]
    block = (width, cols)
    vmem = pl.BlockSpec(memory_space=pltpu.VMEM)
    kinds = len(MOVES)
    return pl.pallas_call(
        functools.partial(exchange_kernel, nb // groups_dev, sectors),
        out_shape=[jax.ShapeDtypeStruct((CAP, *block), jnp.bfloat16)] * kinds
        + [jax.ShapeDtypeStruct(table.shape, jnp.int32)] * kinds
        + [
            jax.ShapeDtypeStruct((owned, *block), jnp.bfloat16),
            jax.ShapeDtypeStruct((owned, width // 4 + width // 16, width), jnp.bfloat16),
        ],
        in_specs=[HBM] * (FIRST + 4) + [vmem],
        out_specs=[HBM] * (2 * kinds + 1) + [vmem],
        scratch_shapes=[
            pltpu.SMEM(table.shape, jnp.int32),
            pltpu.SMEM((nb,), jnp.int32),
            pltpu.VMEM(weights.shape, jnp.bfloat16),
            pltpu.VMEM(fields.shape, jnp.bfloat16),
            pltpu.VMEM((groups_dev, *block), jnp.bfloat16),
            pltpu.VMEM((owned, *block), jnp.bfloat16),
            pltpu.VMEM((CAP, *block), jnp.bfloat16),
            pltpu.VMEM((CAP, *block), jnp.bfloat16),
            pltpu.SemaphoreType.DMA((2 * kinds,)),
            pltpu.SemaphoreType.DMA((2 * kinds,)),
            pltpu.SemaphoreType.DMA((2,)),
            pltpu.SemaphoreType.DMA((groups_dev // CHUNK,)),
            pltpu.SemaphoreType.DMA((4,)),
            pltpu.SemaphoreType.DMA,
        ],
        compiler_params=pltpu.CompilerParams(
            collective_id=0, has_side_effects=True, vmem_limit_bytes=60 * 2**20
        ),
        name="exchange",
    )(*sends, table, source_block, weights, fields, area)


def combine_kernel(row, *refs):
    tables, received_hbm, own, pool = refs[:4], refs[4:8], refs[8], refs[9]
    ten, nine, eight = refs[10:13]
    slots, received, acc, sem = refs[13:17], refs[17:21], refs[21], refs[22]

    @pl.when(pl.program_id(0) == 0)
    def _():
        copies = [
            pltpu.make_async_copy(table, slots[k], sem.at[k]) for k, table in enumerate(tables)
        ] + [
            pltpu.make_async_copy(part, received[k], sem.at[4 + k])
            for k, part in enumerate(received_hbm)
        ]
        for copy in copies:
            copy.start()
        for copy in copies:
            copy.wait()

    base = pl.program_id(0) * STEP
    n9 = nine.shape[1]
    for j in range(STEP):
        acc[j] = own[j].astype(jnp.float32)
    for j in range(STEP):
        for k in range(4):
            slot = slots[k][k * row + base + j]

            @pl.when(slot >= 0)
            def _():
                acc[j] += received[k][slot].astype(jnp.float32)

    for j in range(STEP):
        rounded = acc[j].astype(jnp.bfloat16)
        ten[j] = rounded
        means = jnp.dot(pool[j], rounded, preferred_element_type=jnp.float32)
        nine[j] = means[:n9]
        eight[j] = means[n9:]


def combine(tables, own, received, pool):
    owned, width, cols = own.shape
    n9, n8 = width // 4, width // 16

    def rows(n):
        return pl.BlockSpec((STEP, n, cols), lambda i: (i, 0, 0))

    return pl.pallas_call(
        functools.partial(combine_kernel, table_size(owned)[0]),
        grid=(owned // STEP,),
        out_shape=[
            jax.ShapeDtypeStruct((owned, width, cols), jnp.bfloat16),
            jax.ShapeDtypeStruct((owned, n9, cols), jnp.float32),
            jax.ShapeDtypeStruct((owned, n8, cols), jnp.float32),
        ],
        in_specs=[HBM] * 8
        + [rows(width)]
        + [pl.BlockSpec((STEP, n9 + n8, width), lambda i: (i, 0, 0))],
        out_specs=[rows(width), rows(n9), rows(n8)],
        scratch_shapes=[pltpu.SMEM(tables[0].shape, jnp.int32)] * 4
        + [pltpu.VMEM(received[0].shape, jnp.bfloat16)] * 4
        + [pltpu.VMEM((STEP, width, cols), jnp.float32), pltpu.SemaphoreType.DMA((8,))],
        compiler_params=pltpu.CompilerParams(vmem_limit_bytes=60 * 2**20),
        name="combine",
    )(*tables, *received, own, pool)


def per_device(fields, weights, source_block, target_block, area):
    width = weights.shape[1]
    cols = fields.shape[1]
    owned = area.shape[0] // width
    sectors = lax.axis_size("sector")
    groups_dev = target_block.shape[0]
    blocks = fields.reshape(-1, width, cols)
    sent = outgoing(blocks, weights, source_block, target_block, owned, sectors)
    arrived = exchange(
        sent[:FIRST], sent[FIRST], blocks, weights, source_block, area.reshape(owned, width), sectors,
        groups_dev,
    )
    ten, nine, eight = combine(arrived[4:8], arrived[8], arrived[:4], arrived[9])
    return ten.reshape(-1, cols), nine.reshape(-1, cols), eight.reshape(-1, cols)


def solution(mesh):
    in_specs = (
        P(("groups", "sector"), None),
        P("sector", None, None),
        P("sector"),
        P("sector"),
        P("sector"),
    )
    out_specs = (P(("groups", "sector"), None),) * 3
    return jax.shard_map(
        per_device, mesh=mesh, in_specs=in_specs, out_specs=out_specs, check_vma=False
    )
```

```python
import functools

import jax
import jax.numpy as jnp
from jax import lax
from jax.experimental import pallas as pl
from jax.experimental.pallas import tpu as pltpu
from jax.sharding import PartitionSpec as P

CAP = 16
MOVES = (2, -2, 1, -1)
CHUNK = 8
STEP = 16
FIRST = 2
LANES = 128
HBM = pl.BlockSpec(memory_space=pl.ANY)


def product(wbuf, fbuf, source, w_first, s_first, per_group):
    left = jnp.concatenate([wbuf[w_first + q] for q in range(per_group)], axis=1)
    right = jnp.concatenate(
        [fbuf[source[s_first + q]] for q in range(per_group)], axis=0
    )
    value = jnp.dot(left, right, preferred_element_type=jnp.float32)
    return value.astype(jnp.bfloat16)


def field_copies(f_hbm, fbuf, f_sem, parts):
    rows = fbuf.shape[0] // parts
    return [
        pltpu.make_async_copy(
            f_hbm.at[pl.ds(i * rows, rows)], fbuf.at[pl.ds(i * rows, rows)], f_sem.at[i]
        )
        for i in range(parts)
    ]


def table_size(owned):
    width = -(-owned // LANES) * LANES
    return width, (len(MOVES) + 1) * width, -(-(len(MOVES) * CAP + 1) // LANES) * LANES


def outgoing_kernel(sectors, owned, per_group, source_hbm, target_hbm, w_hbm, f_hbm, *rest):
    sends, table_out = rest[:FIRST], rest[FIRST]
    source, target, table, wbuf, fbuf, obuf, count, i_sem, w_sem, f_sem, o_sem = rest[FIRST + 1 :]
    groups_dev = target.shape[0]
    kinds = len(MOVES)
    width, chosen, _ = table_size(owned)
    index_copies = [
        pltpu.make_async_copy(target_hbm, target, i_sem.at[0]),
        pltpu.make_async_copy(source_hbm, source, i_sem.at[1]),
    ]
    for copy in index_copies:
        copy.start()
    fields_in = field_copies(f_hbm, fbuf, f_sem, f_sem.shape[0])
    for copy in fields_in:
        copy.start()
    me = lax.axis_index("sector")
    for k in range(kinds + 1):
        count[k] = 0

    @pl.loop(0, owned, unroll=8)
    def _(t):
        for k in range(kinds + 1):
            table[k * width + t] = -1

    @pl.loop(0, kinds * CAP, unroll=8)
    def _(t):
        table[chosen + t] = 0

    def w_copy(g, slot):
        return pltpu.make_async_copy(
            w_hbm.at[pl.ds(g * per_group, per_group)],
            wbuf.at[pl.ds(slot * per_group, per_group)],
            w_sem.at[slot],
        )

    for copy in index_copies:
        copy.wait()

    @pl.loop(0, groups_dev, unroll=4)
    def _(g):
        where_to = target[g]
        owner = where_to // owned
        local = where_to - owner * owned
        distance = owner - me
        distance = jnp.where(distance < 0, distance + sectors, distance)
        kind = kinds
        for k, move in enumerate(MOVES):
            kind = jnp.where(distance == move % sectors, k, kind)
        rank = count[kind]
        count[kind] = rank + 1
        mine = kind == kinds
        slot = kind * CAP + jnp.where(mine, 0, rank)
        table[chosen + slot] = g
        table[kind * width + local] = jnp.where(mine, g, rank)

        @pl.when(kind < FIRST)
        def _():
            w_copy(g, slot).start()

    table_copy = pltpu.make_async_copy(table, table_out, o_sem.at[FIRST])
    table_copy.start()
    for copy in fields_in:
        copy.wait()

    unroll = 4
    copies = [table_copy]
    for k in range(FIRST):

        @pl.loop(0, (count[k] + unroll - 1) // unroll)
        def _(step):
            for r in range(unroll):
                rank = step * unroll + r
                slot = k * CAP + rank

                @pl.when(rank < count[k])
                def _():
                    w_copy(table[chosen + slot], slot).wait()

            for r in range(unroll):
                slot = k * CAP + step * unroll + r
                g = table[chosen + slot]
                obuf[slot] = product(
                    wbuf, fbuf, source, slot * per_group, g * per_group, per_group
                )

        copy = pltpu.make_async_copy(obuf.at[pl.ds(CAP * k, CAP)], sends[k], o_sem.at[k])
        copy.start()
        copies.append(copy)
    for copy in copies:
        copy.wait()


def outgoing(fields, weights, source_block, target_block, owned, sectors):
    nb, width, _ = weights.shape
    cols = fields.shape[-1]
    groups_dev = target_block.shape[0]
    per_group = nb // groups_dev
    block = (width, cols)
    _, chosen, tail = table_size(owned)
    return pl.pallas_call(
        functools.partial(outgoing_kernel, sectors, owned, per_group),
        out_shape=[jax.ShapeDtypeStruct((CAP, *block), jnp.bfloat16)] * FIRST
        + [jax.ShapeDtypeStruct((chosen + tail,), jnp.int32)],
        in_specs=[HBM] * 4,
        out_specs=[HBM] * (FIRST + 1),
        scratch_shapes=[
            pltpu.SMEM((nb,), jnp.int32),
            pltpu.SMEM((groups_dev,), jnp.int32),
            pltpu.SMEM((chosen + tail,), jnp.int32),
            pltpu.VMEM((FIRST * CAP * per_group, width, width), jnp.bfloat16),
            pltpu.VMEM(fields.shape, jnp.bfloat16),
            pltpu.VMEM((FIRST * CAP, *block), jnp.bfloat16),
            pltpu.SMEM((len(MOVES) + 1,), jnp.int32),
            pltpu.SemaphoreType.DMA((2,)),
            pltpu.SemaphoreType.DMA((FIRST * CAP,)),
            pltpu.SemaphoreType.DMA((4,)),
            pltpu.SemaphoreType.DMA((FIRST + 1,)),
        ],
        compiler_params=pltpu.CompilerParams(vmem_limit_bytes=60 * 2**20),
        name="outgoing",
    )(source_block, target_block, weights, fields)


def exchange_kernel(per_group, sectors, *refs):
    sends, table_hbm = refs[:FIRST], refs[FIRST]
    source_hbm, w_hbm, f_hbm, area = refs[FIRST + 1 : FIRST + 5]
    rest = refs[FIRST + 5 :]
    received, tables_out, own_out, pool = rest[:4], rest[4:8], rest[8], rest[9]
    table, source, wbuf, fbuf, pbuf, obuf, near0, near1 = rest[10:18]
    send_sem, recv_sem, i_sem, w_sem, f_sem, o_sem = rest[18:]
    near = (near0, near1)
    me = lax.axis_index("sector")
    kinds = len(MOVES)
    chunks = w_sem.shape[0]
    per_chunk = CHUNK * per_group
    owned = obuf.shape[0]
    own_row, chosen, _ = table_size(owned)
    own_row = kinds * own_row
    local = [
        pltpu.make_async_copy(table_hbm, table, i_sem.at[0]),
        pltpu.make_async_copy(source_hbm, source, i_sem.at[1]),
    ] + field_copies(f_hbm, fbuf, f_sem, f_sem.shape[0])
    peers = [{"sector": lax.rem(me + sectors + move, sectors)} for move in MOVES]
    barrier = pltpu.get_barrier_semaphore()
    for peer in peers:
        pl.semaphore_signal(
            barrier, inc=1, device_id=peer, device_id_type=pl.DeviceIdType.MESH
        )
    for copy in local:
        copy.start()

    def w_copy(c):
        rows = pl.ds(c * per_chunk, per_chunk)
        return pltpu.make_async_copy(w_hbm.at[rows], wbuf.at[rows], w_sem.at[c])

    pl.semaphore_wait(barrier, kinds)

    def remote(index, k, source_ref, target_ref):
        return pltpu.make_async_remote_copy(
            src_ref=source_ref,
            dst_ref=target_ref,
            send_sem=send_sem.at[index],
            recv_sem=recv_sem.at[index],
            device_id=peers[k],
            device_id_type=pl.DeviceIdType.MESH,
        )

    moved = [remote(k, k, sends[k], received[k]) for k in range(FIRST)]
    moved += [remote(kinds + k, k, table_hbm, tables_out[k]) for k in range(kinds)]
    for copy in moved:
        copy.start()
    for c in range(chunks):
        w_copy(c).start()
    for copy in local:
        copy.wait()

    @pl.loop(0, chunks)
    def _(c):
        w_copy(c).wait()

        @pl.loop(0, CHUNK // 4)
        def _(step):
            for p in range(4):
                g = c * CHUNK + step * 4 + p
                pbuf[g] = product(wbuf, fbuf, source, g * per_group, g * per_group, per_group)

    for k in range(FIRST, kinds):

        @pl.loop(0, CAP)
        def _(rank):
            near[k - FIRST][rank] = pbuf[table[chosen + k * CAP + rank]]

        moved.append(remote(k, k, near[k - FIRST], received[k]))
        moved[-1].start()

    @pl.loop(0, owned)
    def _(t):
        g = table[own_row + t]
        value = pbuf[jnp.maximum(g, 0)]
        obuf[t] = jnp.where(g >= 0, value.astype(jnp.float32), 0.0).astype(obuf.dtype)

    out = pltpu.make_async_copy(obuf, own_out, o_sem)
    out.start()
    width = area.shape[1]
    rows = pool.shape[1]
    n9 = width // 4
    row = lax.broadcasted_iota(jnp.int32, (rows, width), 0)
    pixel = lax.broadcasted_iota(jnp.int32, (rows, width), 1)
    member = jnp.where(row < n9, pixel // 4 - row, pixel // 16 - (row - n9)) == 0

    @pl.loop(0, owned)
    def _(t):
        share = jnp.where(member, area[pl.ds(t, 1), :], 0.0)
        pool[t] = (share / share.sum(1, keepdims=True)).astype(pool.dtype)

    out.wait()
    for copy in moved:
        copy.wait()


def exchange(sends, table, fields, weights, source_block, area, sectors, groups_dev):
    nb, width, _ = weights.shape
    cols = fields.shape[-1]
    owned = area.shape[0]
    block = (width, cols)
    vmem = pl.BlockSpec(memory_space=pltpu.VMEM)
    kinds = len(MOVES)
    return pl.pallas_call(
        functools.partial(exchange_kernel, nb // groups_dev, sectors),
        out_shape=[jax.ShapeDtypeStruct((CAP, *block), jnp.bfloat16)] * kinds
        + [jax.ShapeDtypeStruct(table.shape, jnp.int32)] * kinds
        + [
            jax.ShapeDtypeStruct((owned, *block), jnp.bfloat16),
            jax.ShapeDtypeStruct((owned, width // 4 + width // 16, width), jnp.bfloat16),
        ],
        in_specs=[HBM] * (FIRST + 4) + [vmem],
        out_specs=[HBM] * (2 * kinds + 1) + [vmem],
        scratch_shapes=[
            pltpu.SMEM(table.shape, jnp.int32),
            pltpu.SMEM((nb,), jnp.int32),
            pltpu.VMEM(weights.shape, jnp.bfloat16),
            pltpu.VMEM(fields.shape, jnp.bfloat16),
            pltpu.VMEM((groups_dev, *block), jnp.bfloat16),
            pltpu.VMEM((owned, *block), jnp.bfloat16),
            pltpu.VMEM((CAP, *block), jnp.bfloat16),
            pltpu.VMEM((CAP, *block), jnp.bfloat16),
            pltpu.SemaphoreType.DMA((2 * kinds,)),
            pltpu.SemaphoreType.DMA((2 * kinds,)),
            pltpu.SemaphoreType.DMA((2,)),
            pltpu.SemaphoreType.DMA((groups_dev // CHUNK,)),
            pltpu.SemaphoreType.DMA((4,)),
            pltpu.SemaphoreType.DMA,
        ],
        compiler_params=pltpu.CompilerParams(
            collective_id=0, has_side_effects=True, vmem_limit_bytes=60 * 2**20
        ),
        name="exchange",
    )(*sends, table, source_block, weights, fields, area)


def combine_kernel(row, *refs):
    tables, received_hbm, own_hbm, pool_hbm = refs[:4], refs[4:8], refs[8], refs[9]
    outs_hbm = refs[10:13]
    slots, received, own, pool = refs[13:17], refs[17:21], refs[21], refs[22]
    outs, sem, own_sem, pool_sem, out_sem = refs[23:26], refs[26], refs[27], refs[28], refs[29]
    ten, nine, eight = outs
    chunks = own_sem.shape[0]
    step = own.shape[0] // chunks
    n9 = nine.shape[1]

    def part(source, place, c, semaphore):
        rows = pl.ds(c * step, step)
        return pltpu.make_async_copy(source.at[rows], place.at[rows], semaphore)

    def results(c):
        return [part(outs[i], outs_hbm[i], c, out_sem.at[3 * c + i]) for i in range(3)]

    copies = [
        pltpu.make_async_copy(table, slots[k], sem.at[k]) for k, table in enumerate(tables)
    ] + [
        pltpu.make_async_copy(block, received[k], sem.at[4 + k])
        for k, block in enumerate(received_hbm)
    ]
    for copy in copies:
        copy.start()
    for c in range(chunks):
        part(own_hbm, own, c, own_sem.at[c]).start()
        part(pool_hbm, pool, c, pool_sem.at[c]).start()
    for copy in copies:
        copy.wait()

    @pl.loop(0, chunks)
    def _(c):
        part(own_hbm, own, c, own_sem.at[c]).wait()
        part(pool_hbm, pool, c, pool_sem.at[c]).wait()
        for j in range(step):
            t = c * step + j
            total = own[t].astype(jnp.float32)
            for k in range(4):
                slot = slots[k][k * row + t]
                value = received[k][jnp.maximum(slot, 0)].astype(jnp.float32)
                total = total + jnp.where(slot >= 0, value, 0.0)
            rounded = total.astype(jnp.bfloat16)
            ten[t] = rounded
            means = jnp.dot(pool[t], rounded, preferred_element_type=jnp.float32)
            nine[t] = means[:n9]
            eight[t] = means[n9:]
        for copy in results(c):
            copy.start()

    @pl.loop(0, chunks)
    def _(c):
        for copy in results(c):
            copy.wait()


def combine(tables, own, received, pool):
    owned, width, cols = own.shape
    chunks = owned // STEP
    outs = [
        jax.ShapeDtypeStruct((owned, width, cols), jnp.bfloat16),
        jax.ShapeDtypeStruct((owned, width // 4, cols), jnp.float32),
        jax.ShapeDtypeStruct((owned, width // 16, cols), jnp.float32),
    ]
    return pl.pallas_call(
        functools.partial(combine_kernel, table_size(owned)[0]),
        out_shape=outs,
        in_specs=[HBM] * 10,
        out_specs=[HBM] * 3,
        scratch_shapes=[pltpu.SMEM(tables[0].shape, jnp.int32)] * 4
        + [pltpu.VMEM(received[0].shape, jnp.bfloat16)] * 4
        + [pltpu.VMEM(own.shape, jnp.bfloat16), pltpu.VMEM(pool.shape, jnp.bfloat16)]
        + [pltpu.VMEM(out.shape, out.dtype) for out in outs]
        + [
            pltpu.SemaphoreType.DMA((8,)),
            pltpu.SemaphoreType.DMA((chunks,)),
            pltpu.SemaphoreType.DMA((chunks,)),
            pltpu.SemaphoreType.DMA((3 * chunks,)),
        ],
        compiler_params=pltpu.CompilerParams(vmem_limit_bytes=60 * 2**20),
        name="combine",
    )(*tables, *received, own, pool)


def per_device(fields, weights, source_block, target_block, area):
    width = weights.shape[1]
    cols = fields.shape[1]
    owned = area.shape[0] // width
    sectors = lax.axis_size("sector")
    groups_dev = target_block.shape[0]
    blocks = fields.reshape(-1, width, cols)
    sent = outgoing(blocks, weights, source_block, target_block, owned, sectors)
    arrived = exchange(
        sent[:FIRST], sent[FIRST], blocks, weights, source_block, area.reshape(owned, width), sectors,
        groups_dev,
    )
    ten, nine, eight = combine(arrived[4:8], arrived[8], arrived[:4], arrived[9])
    return ten.reshape(-1, cols), nine.reshape(-1, cols), eight.reshape(-1, cols)


def solution(mesh):
    in_specs = (
        P(("groups", "sector"), None),
        P("sector", None, None),
        P("sector"),
        P("sector"),
        P("sector"),
    )
    out_specs = (P(("groups", "sector"), None),) * 3
    return jax.shard_map(
        per_device, mesh=mesh, in_specs=in_specs, out_specs=out_specs, check_vma=False
    )
```

```python
import functools

import jax
import jax.numpy as jnp
from jax import lax
from jax.experimental import pallas as pl
from jax.experimental.pallas import tpu as pltpu
from jax.sharding import PartitionSpec as P

CAP = 16
MOVES = (2, -2, 1, -1)
CHUNK = 8
STEP = 16
FIRST = 2
HEAD = 8
LANES = 128
HBM = pl.BlockSpec(memory_space=pl.ANY)


def product(wbuf, fbuf, source, w_first, s_first, per_group):
    left = jnp.concatenate([wbuf[w_first + q] for q in range(per_group)], axis=1)
    right = jnp.concatenate(
        [fbuf[source[s_first + q]] for q in range(per_group)], axis=0
    )
    value = jnp.dot(left, right, preferred_element_type=jnp.float32)
    return value.astype(jnp.bfloat16)


def field_copies(f_hbm, fbuf, f_sem, parts):
    rows = fbuf.shape[0] // parts
    return [
        pltpu.make_async_copy(
            f_hbm.at[pl.ds(i * rows, rows)], fbuf.at[pl.ds(i * rows, rows)], f_sem.at[i]
        )
        for i in range(parts)
    ]


def table_size(owned):
    width = -(-owned // LANES) * LANES
    return width, (len(MOVES) + 1) * width, -(-(len(MOVES) * CAP + 1) // LANES) * LANES


def outgoing_kernel(sectors, owned, per_group, source_hbm, target_hbm, w_hbm, f_hbm, *rest):
    sends, table_out = rest[:FIRST], rest[FIRST]
    source, target, table, wbuf, fbuf, obuf, count, i_sem, w_sem, f_sem, o_sem = rest[FIRST + 1 :]
    groups_dev = target.shape[0]
    kinds = len(MOVES)
    width, chosen, _ = table_size(owned)
    index_copies = [
        pltpu.make_async_copy(target_hbm, target, i_sem.at[0]),
        pltpu.make_async_copy(source_hbm, source, i_sem.at[1]),
    ]
    for copy in index_copies:
        copy.start()
    fields_in = field_copies(f_hbm, fbuf, f_sem, f_sem.shape[0])
    for copy in fields_in:
        copy.start()
    me = lax.axis_index("sector")
    for k in range(kinds + 1):
        count[k] = 0

    @pl.loop(0, owned, unroll=8)
    def _(t):
        for k in range(kinds + 1):
            table[k * width + t] = -1

    @pl.loop(0, kinds * CAP, unroll=8)
    def _(t):
        table[chosen + t] = 0

    def w_copy(g, slot):
        return pltpu.make_async_copy(
            w_hbm.at[pl.ds(g * per_group, per_group)],
            wbuf.at[pl.ds(slot * per_group, per_group)],
            w_sem.at[slot],
        )

    for copy in index_copies:
        copy.wait()

    @pl.loop(0, groups_dev, unroll=4)
    def _(g):
        where_to = target[g]
        owner = where_to // owned
        local = where_to - owner * owned
        distance = owner - me
        distance = jnp.where(distance < 0, distance + sectors, distance)
        kind = kinds
        for k, move in enumerate(MOVES):
            kind = jnp.where(distance == move % sectors, k, kind)
        rank = count[kind]
        count[kind] = rank + 1
        mine = kind == kinds
        slot = kind * CAP + jnp.where(mine, 0, rank)
        table[chosen + slot] = g
        table[kind * width + local] = jnp.where(mine, g, rank)

        @pl.when((kind < FIRST) & (rank < HEAD))
        def _():
            w_copy(g, kind * HEAD + rank).start()

    table_copy = pltpu.make_async_copy(table, table_out, o_sem.at[FIRST])
    table_copy.start()
    for copy in fields_in:
        copy.wait()

    unroll = HEAD // 2
    copies = [table_copy]
    for k in range(FIRST):

        @pl.loop(0, (jnp.minimum(count[k], HEAD) + unroll - 1) // unroll)
        def _(step):
            for r in range(unroll):
                rank = step * unroll + r

                @pl.when(rank < count[k])
                def _():
                    w_copy(table[chosen + k * CAP + rank], k * HEAD + rank).wait()

            for r in range(unroll):
                rank = step * unroll + r
                slot = k * HEAD + rank
                g = table[chosen + k * CAP + rank]
                obuf[slot] = product(
                    wbuf, fbuf, source, slot * per_group, g * per_group, per_group
                )

        copy = pltpu.make_async_copy(obuf.at[pl.ds(HEAD * k, HEAD)], sends[k], o_sem.at[k])
        copy.start()
        copies.append(copy)
    for copy in copies:
        copy.wait()


def outgoing(fields, weights, source_block, target_block, owned, sectors):
    nb, width, _ = weights.shape
    cols = fields.shape[-1]
    groups_dev = target_block.shape[0]
    per_group = nb // groups_dev
    block = (width, cols)
    _, chosen, tail = table_size(owned)
    return pl.pallas_call(
        functools.partial(outgoing_kernel, sectors, owned, per_group),
        out_shape=[jax.ShapeDtypeStruct((HEAD, *block), jnp.bfloat16)] * FIRST
        + [jax.ShapeDtypeStruct((chosen + tail,), jnp.int32)],
        in_specs=[HBM] * 4,
        out_specs=[HBM] * (FIRST + 1),
        scratch_shapes=[
            pltpu.SMEM((nb,), jnp.int32),
            pltpu.SMEM((groups_dev,), jnp.int32),
            pltpu.SMEM((chosen + tail,), jnp.int32),
            pltpu.VMEM((FIRST * HEAD * per_group, width, width), jnp.bfloat16),
            pltpu.VMEM(fields.shape, jnp.bfloat16),
            pltpu.VMEM((FIRST * HEAD, *block), jnp.bfloat16),
            pltpu.SMEM((len(MOVES) + 1,), jnp.int32),
            pltpu.SemaphoreType.DMA((2,)),
            pltpu.SemaphoreType.DMA((FIRST * HEAD,)),
            pltpu.SemaphoreType.DMA((4,)),
            pltpu.SemaphoreType.DMA((FIRST + 1,)),
        ],
        compiler_params=pltpu.CompilerParams(vmem_limit_bytes=60 * 2**20),
        name="outgoing",
    )(source_block, target_block, weights, fields)


def exchange_kernel(per_group, sectors, *refs):
    sends, table_hbm = refs[:FIRST], refs[FIRST]
    source_hbm, w_hbm, f_hbm, area = refs[FIRST + 1 : FIRST + 5]
    rest = refs[FIRST + 5 :]
    received, tables_out, own_out, pool = rest[:4], rest[4:8], rest[8], rest[9]
    table, source, wbuf, fbuf, pbuf, obuf = rest[10:16]
    later = rest[16:20]
    send_sem, recv_sem, i_sem, w_sem, f_sem, o_sem = rest[20:]
    me = lax.axis_index("sector")
    kinds = len(MOVES)
    chunks = w_sem.shape[0]
    per_chunk = CHUNK * per_group
    owned = obuf.shape[0]
    own_row, chosen, _ = table_size(owned)
    own_row = kinds * own_row
    local = [
        pltpu.make_async_copy(table_hbm, table, i_sem.at[0]),
        pltpu.make_async_copy(source_hbm, source, i_sem.at[1]),
    ] + field_copies(f_hbm, fbuf, f_sem, f_sem.shape[0])
    peers = [{"sector": lax.rem(me + sectors + move, sectors)} for move in MOVES]
    barrier = pltpu.get_barrier_semaphore()
    for peer in peers:
        pl.semaphore_signal(
            barrier, inc=1, device_id=peer, device_id_type=pl.DeviceIdType.MESH
        )
    for copy in local:
        copy.start()

    def w_copy(c):
        rows = pl.ds(c * per_chunk, per_chunk)
        return pltpu.make_async_copy(w_hbm.at[rows], wbuf.at[rows], w_sem.at[c])

    pl.semaphore_wait(barrier, kinds)

    def remote(index, k, source_ref, target_ref):
        return pltpu.make_async_remote_copy(
            src_ref=source_ref,
            dst_ref=target_ref,
            send_sem=send_sem.at[index],
            recv_sem=recv_sem.at[index],
            device_id=peers[k],
            device_id_type=pl.DeviceIdType.MESH,
        )

    moved = [remote(k, k, sends[k], received[k].at[pl.ds(0, HEAD)]) for k in range(FIRST)]
    moved += [remote(kinds + k, k, table_hbm, tables_out[k]) for k in range(kinds)]
    for copy in moved:
        copy.start()
    for c in range(chunks):
        w_copy(c).start()
    for copy in local:
        copy.wait()

    @pl.loop(0, chunks)
    def _(c):
        w_copy(c).wait()

        @pl.loop(0, CHUNK // 4)
        def _(step):
            for p in range(4):
                g = c * CHUNK + step * 4 + p
                pbuf[g] = product(wbuf, fbuf, source, g * per_group, g * per_group, per_group)

    for k in range(kinds):
        done = HEAD if k < FIRST else 0

        @pl.loop(0, CAP - done)
        def _(i):
            later[k][i] = pbuf[table[chosen + k * CAP + done + i]]

        rows = pl.ds(done, CAP - done)
        moved.append(remote(2 * kinds + k, k, later[k], received[k].at[rows]))
        moved[-1].start()

    @pl.loop(0, owned)
    def _(t):
        g = table[own_row + t]
        value = pbuf[jnp.maximum(g, 0)]
        obuf[t] = jnp.where(g >= 0, value.astype(jnp.float32), 0.0).astype(obuf.dtype)

    out = pltpu.make_async_copy(obuf, own_out, o_sem)
    out.start()
    width = area.shape[1]
    rows = pool.shape[1]
    n9 = width // 4
    row = lax.broadcasted_iota(jnp.int32, (rows, width), 0)
    pixel = lax.broadcasted_iota(jnp.int32, (rows, width), 1)
    member = jnp.where(row < n9, pixel // 4 - row, pixel // 16 - (row - n9)) == 0

    @pl.loop(0, owned)
    def _(t):
        share = jnp.where(member, area[pl.ds(t, 1), :], 0.0)
        pool[t] = (share / share.sum(1, keepdims=True)).astype(pool.dtype)

    out.wait()
    for copy in moved:
        copy.wait()


def exchange(sends, table, fields, weights, source_block, area, sectors, groups_dev):
    nb, width, _ = weights.shape
    cols = fields.shape[-1]
    owned = area.shape[0]
    block = (width, cols)
    vmem = pl.BlockSpec(memory_space=pltpu.VMEM)
    kinds = len(MOVES)
    return pl.pallas_call(
        functools.partial(exchange_kernel, nb // groups_dev, sectors),
        out_shape=[jax.ShapeDtypeStruct((CAP, *block), jnp.bfloat16)] * kinds
        + [jax.ShapeDtypeStruct(table.shape, jnp.int32)] * kinds
        + [
            jax.ShapeDtypeStruct((owned, *block), jnp.bfloat16),
            jax.ShapeDtypeStruct((owned, width // 4 + width // 16, width), jnp.bfloat16),
        ],
        in_specs=[HBM] * (FIRST + 4) + [vmem],
        out_specs=[HBM] * (2 * kinds + 1) + [vmem],
        scratch_shapes=[
            pltpu.SMEM(table.shape, jnp.int32),
            pltpu.SMEM((nb,), jnp.int32),
            pltpu.VMEM(weights.shape, jnp.bfloat16),
            pltpu.VMEM(fields.shape, jnp.bfloat16),
            pltpu.VMEM((groups_dev, *block), jnp.bfloat16),
            pltpu.VMEM((owned, *block), jnp.bfloat16),
        ]
        + [
            pltpu.VMEM((CAP - (HEAD if k < FIRST else 0), *block), jnp.bfloat16)
            for k in range(kinds)
        ]
        + [
            pltpu.SemaphoreType.DMA((3 * kinds,)),
            pltpu.SemaphoreType.DMA((3 * kinds,)),
            pltpu.SemaphoreType.DMA((2,)),
            pltpu.SemaphoreType.DMA((groups_dev // CHUNK,)),
            pltpu.SemaphoreType.DMA((4,)),
            pltpu.SemaphoreType.DMA,
        ],
        compiler_params=pltpu.CompilerParams(
            collective_id=0, has_side_effects=True, vmem_limit_bytes=60 * 2**20
        ),
        name="exchange",
    )(*sends, table, source_block, weights, fields, area)


def combine_kernel(row, *refs):
    tables, received_hbm, own_hbm, pool_hbm = refs[:4], refs[4:8], refs[8], refs[9]
    outs_hbm = refs[10:13]
    slots, received, own, pool = refs[13:17], refs[17:21], refs[21], refs[22]
    outs, sem, own_sem, pool_sem, out_sem = refs[23:26], refs[26], refs[27], refs[28], refs[29]
    ten, nine, eight = outs
    chunks = own_sem.shape[0]
    step = own.shape[0] // chunks
    n9 = nine.shape[1]

    def part(source, place, c, semaphore):
        rows = pl.ds(c * step, step)
        return pltpu.make_async_copy(source.at[rows], place.at[rows], semaphore)

    def results(c):
        return [part(outs[i], outs_hbm[i], c, out_sem.at[3 * c + i]) for i in range(3)]

    copies = [
        pltpu.make_async_copy(table, slots[k], sem.at[k]) for k, table in enumerate(tables)
    ] + [
        pltpu.make_async_copy(block, received[k], sem.at[4 + k])
        for k, block in enumerate(received_hbm)
    ]
    for copy in copies:
        copy.start()
    for c in range(chunks):
        part(own_hbm, own, c, own_sem.at[c]).start()
        part(pool_hbm, pool, c, pool_sem.at[c]).start()
    for copy in copies:
        copy.wait()

    @pl.loop(0, chunks)
    def _(c):
        part(own_hbm, own, c, own_sem.at[c]).wait()
        part(pool_hbm, pool, c, pool_sem.at[c]).wait()
        for j in range(step):
            t = c * step + j
            total = own[t].astype(jnp.float32)
            for k in range(4):
                slot = slots[k][k * row + t]
                value = received[k][jnp.maximum(slot, 0)].astype(jnp.float32)
                total = total + jnp.where(slot >= 0, value, 0.0)
            rounded = total.astype(jnp.bfloat16)
            ten[t] = rounded
            means = jnp.dot(pool[t], rounded, preferred_element_type=jnp.float32)
            nine[t] = means[:n9]
            eight[t] = means[n9:]
        for copy in results(c):
            copy.start()

    @pl.loop(0, chunks)
    def _(c):
        for copy in results(c):
            copy.wait()


def combine(tables, own, received, pool):
    owned, width, cols = own.shape
    chunks = owned // STEP
    outs = [
        jax.ShapeDtypeStruct((owned, width, cols), jnp.bfloat16),
        jax.ShapeDtypeStruct((owned, width // 4, cols), jnp.float32),
        jax.ShapeDtypeStruct((owned, width // 16, cols), jnp.float32),
    ]
    return pl.pallas_call(
        functools.partial(combine_kernel, table_size(owned)[0]),
        out_shape=outs,
        in_specs=[HBM] * 10,
        out_specs=[HBM] * 3,
        scratch_shapes=[pltpu.SMEM(tables[0].shape, jnp.int32)] * 4
        + [pltpu.VMEM(received[0].shape, jnp.bfloat16)] * 4
        + [pltpu.VMEM(own.shape, jnp.bfloat16), pltpu.VMEM(pool.shape, jnp.bfloat16)]
        + [pltpu.VMEM(out.shape, out.dtype) for out in outs]
        + [
            pltpu.SemaphoreType.DMA((8,)),
            pltpu.SemaphoreType.DMA((chunks,)),
            pltpu.SemaphoreType.DMA((chunks,)),
            pltpu.SemaphoreType.DMA((3 * chunks,)),
        ],
        compiler_params=pltpu.CompilerParams(vmem_limit_bytes=60 * 2**20),
        name="combine",
    )(*tables, *received, own, pool)


def per_device(fields, weights, source_block, target_block, area):
    width = weights.shape[1]
    cols = fields.shape[1]
    owned = area.shape[0] // width
    sectors = lax.axis_size("sector")
    groups_dev = target_block.shape[0]
    blocks = fields.reshape(-1, width, cols)
    sent = outgoing(blocks, weights, source_block, target_block, owned, sectors)
    arrived = exchange(
        sent[:FIRST], sent[FIRST], blocks, weights, source_block, area.reshape(owned, width), sectors,
        groups_dev,
    )
    ten, nine, eight = combine(arrived[4:8], arrived[8], arrived[:4], arrived[9])
    return ten.reshape(-1, cols), nine.reshape(-1, cols), eight.reshape(-1, cols)


def solution(mesh):
    in_specs = (
        P(("groups", "sector"), None),
        P("sector", None, None),
        P("sector"),
        P("sector"),
        P("sector"),
    )
    out_specs = (P(("groups", "sector"), None),) * 3
    return jax.shard_map(
        per_device, mesh=mesh, in_specs=in_specs, out_specs=out_specs, check_vma=False
    )
```

```python
import functools

import jax
import jax.numpy as jnp
from jax import lax
from jax.experimental import pallas as pl
from jax.experimental.pallas import tpu as pltpu
from jax.sharding import PartitionSpec as P

CAP = 16
MOVES = (2, -2, 1, -1)
CHUNK = 8
STEP = 16
FIRST = 2
HEAD = 8
LANES = 128
HBM = pl.BlockSpec(memory_space=pl.ANY)


def product(wbuf, fbuf, source, w_first, s_first, per_group):
    left = jnp.concatenate([wbuf[w_first + q] for q in range(per_group)], axis=1)
    right = jnp.concatenate(
        [fbuf[source[s_first + q]] for q in range(per_group)], axis=0
    )
    value = jnp.dot(left, right, preferred_element_type=jnp.float32)
    return value.astype(jnp.bfloat16)


def field_copies(f_hbm, fbuf, f_sem, parts):
    rows = fbuf.shape[0] // parts
    return [
        pltpu.make_async_copy(
            f_hbm.at[pl.ds(i * rows, rows)], fbuf.at[pl.ds(i * rows, rows)], f_sem.at[i]
        )
        for i in range(parts)
    ]


def table_size(owned):
    width = -(-owned // LANES) * LANES
    return width, (len(MOVES) + 1) * width, -(-(len(MOVES) * CAP + 1) // LANES) * LANES


def outgoing_kernel(sectors, owned, per_group, source_hbm, target_hbm, w_hbm, f_hbm, *rest):
    sends, table_out = rest[:FIRST], rest[FIRST]
    source, target, table, wbuf, fbuf, obuf, count, i_sem, w_sem, f_sem, o_sem = rest[FIRST + 1 :]
    groups_dev = target.shape[0]
    kinds = len(MOVES)
    width, chosen, _ = table_size(owned)
    index_copies = [
        pltpu.make_async_copy(target_hbm, target, i_sem.at[0]),
        pltpu.make_async_copy(source_hbm, source, i_sem.at[1]),
    ]
    for copy in index_copies:
        copy.start()
    fields_in = field_copies(f_hbm, fbuf, f_sem, f_sem.shape[0])
    for copy in fields_in:
        copy.start()
    me = lax.axis_index("sector")
    for k in range(kinds + 1):
        count[k] = 0

    @pl.loop(0, owned, unroll=8)
    def _(t):
        for k in range(kinds + 1):
            table[k * width + t] = -1

    @pl.loop(0, kinds * CAP, unroll=8)
    def _(t):
        table[chosen + t] = 0

    def w_copy(g, slot):
        return pltpu.make_async_copy(
            w_hbm.at[pl.ds(g * per_group, per_group)],
            wbuf.at[pl.ds(slot * per_group, per_group)],
            w_sem.at[slot],
        )

    for copy in index_copies:
        copy.wait()

    @pl.loop(0, groups_dev, unroll=4)
    def _(g):
        where_to = target[g]
        owner = where_to // owned
        local = where_to - owner * owned
        distance = owner - me
        distance = jnp.where(distance < 0, distance + sectors, distance)
        kind = kinds
        for k, move in enumerate(MOVES):
            kind = jnp.where(distance == move % sectors, k, kind)
        rank = count[kind]
        count[kind] = rank + 1
        mine = kind == kinds
        slot = kind * CAP + jnp.where(mine, 0, rank)
        table[chosen + slot] = g
        table[kind * width + local] = jnp.where(mine, g, rank)

        @pl.when((kind < FIRST) & (rank < HEAD))
        def _():
            w_copy(g, kind * HEAD + rank).start()

    table_copy = pltpu.make_async_copy(table, table_out, o_sem.at[FIRST])
    table_copy.start()
    for copy in fields_in:
        copy.wait()

    unroll = HEAD
    copies = [table_copy]
    for k in range(FIRST):

        @pl.loop(0, (jnp.minimum(count[k], HEAD) + unroll - 1) // unroll)
        def _(step):
            for r in range(unroll):
                rank = step * unroll + r

                @pl.when(rank < count[k])
                def _():
                    w_copy(table[chosen + k * CAP + rank], k * HEAD + rank).wait()

            for r in range(unroll):
                rank = step * unroll + r
                slot = k * HEAD + rank
                g = table[chosen + k * CAP + rank]
                obuf[slot] = product(
                    wbuf, fbuf, source, slot * per_group, g * per_group, per_group
                )

        copy = pltpu.make_async_copy(obuf.at[pl.ds(HEAD * k, HEAD)], sends[k], o_sem.at[k])
        copy.start()
        copies.append(copy)
    for copy in copies:
        copy.wait()


def outgoing(fields, weights, source_block, target_block, owned, sectors):
    nb, width, _ = weights.shape
    cols = fields.shape[-1]
    groups_dev = target_block.shape[0]
    per_group = nb // groups_dev
    block = (width, cols)
    _, chosen, tail = table_size(owned)
    return pl.pallas_call(
        functools.partial(outgoing_kernel, sectors, owned, per_group),
        out_shape=[jax.ShapeDtypeStruct((HEAD, *block), jnp.bfloat16)] * FIRST
        + [jax.ShapeDtypeStruct((chosen + tail,), jnp.int32)],
        in_specs=[HBM] * 4,
        out_specs=[HBM] * (FIRST + 1),
        scratch_shapes=[
            pltpu.SMEM((nb,), jnp.int32),
            pltpu.SMEM((groups_dev,), jnp.int32),
            pltpu.SMEM((chosen + tail,), jnp.int32),
            pltpu.VMEM((FIRST * HEAD * per_group, width, width), jnp.bfloat16),
            pltpu.VMEM(fields.shape, jnp.bfloat16),
            pltpu.VMEM((FIRST * HEAD, *block), jnp.bfloat16),
            pltpu.SMEM((len(MOVES) + 1,), jnp.int32),
            pltpu.SemaphoreType.DMA((2,)),
            pltpu.SemaphoreType.DMA((FIRST * HEAD,)),
            pltpu.SemaphoreType.DMA((4,)),
            pltpu.SemaphoreType.DMA((FIRST + 1,)),
        ],
        compiler_params=pltpu.CompilerParams(vmem_limit_bytes=60 * 2**20),
        name="outgoing",
    )(source_block, target_block, weights, fields)


def exchange_kernel(per_group, sectors, *refs):
    sends, table_hbm = refs[:FIRST], refs[FIRST]
    source_hbm, w_hbm, f_hbm, area = refs[FIRST + 1 : FIRST + 5]
    rest = refs[FIRST + 5 :]
    received, tables_out, own_out, pool = rest[:4], rest[4:8], rest[8], rest[9]
    table, source, wbuf, fbuf, pbuf, obuf = rest[10:16]
    later = rest[16:20]
    send_sem, recv_sem, i_sem, w_sem, f_sem, o_sem = rest[20:]
    me = lax.axis_index("sector")
    kinds = len(MOVES)
    chunks = w_sem.shape[0]
    per_chunk = CHUNK * per_group
    owned = obuf.shape[0]
    own_row, chosen, _ = table_size(owned)
    own_row = kinds * own_row
    local = [
        pltpu.make_async_copy(table_hbm, table, i_sem.at[0]),
        pltpu.make_async_copy(source_hbm, source, i_sem.at[1]),
    ] + field_copies(f_hbm, fbuf, f_sem, f_sem.shape[0])
    peers = [{"sector": lax.rem(me + sectors + move, sectors)} for move in MOVES]
    barrier = pltpu.get_barrier_semaphore()
    for peer in peers:
        pl.semaphore_signal(
            barrier, inc=1, device_id=peer, device_id_type=pl.DeviceIdType.MESH
        )
    for copy in local:
        copy.start()

    def w_copy(c):
        rows = pl.ds(c * per_chunk, per_chunk)
        return pltpu.make_async_copy(w_hbm.at[rows], wbuf.at[rows], w_sem.at[c])

    pl.semaphore_wait(barrier, kinds)

    def remote(index, k, source_ref, target_ref):
        return pltpu.make_async_remote_copy(
            src_ref=source_ref,
            dst_ref=target_ref,
            send_sem=send_sem.at[index],
            recv_sem=recv_sem.at[index],
            device_id=peers[k],
            device_id_type=pl.DeviceIdType.MESH,
        )

    moved = [remote(k, k, sends[k], received[k].at[pl.ds(0, HEAD)]) for k in range(FIRST)]
    moved += [remote(kinds + k, k, table_hbm, tables_out[k]) for k in range(kinds)]
    for copy in moved:
        copy.start()
    for c in range(chunks):
        w_copy(c).start()
    for copy in local:
        copy.wait()

    @pl.loop(0, chunks)
    def _(c):
        w_copy(c).wait()

        @pl.loop(0, CHUNK // 4)
        def _(step):
            for p in range(4):
                g = c * CHUNK + step * 4 + p
                pbuf[g] = product(wbuf, fbuf, source, g * per_group, g * per_group, per_group)

    for k in range(kinds):
        done = HEAD if k < FIRST else 0

        @pl.loop(0, CAP - done)
        def _(i):
            later[k][i] = pbuf[table[chosen + k * CAP + done + i]]

        rows = pl.ds(done, CAP - done)
        moved.append(remote(2 * kinds + k, k, later[k], received[k].at[rows]))
        moved[-1].start()

    @pl.loop(0, owned)
    def _(t):
        g = table[own_row + t]
        value = pbuf[jnp.maximum(g, 0)]
        obuf[t] = jnp.where(g >= 0, value.astype(jnp.float32), 0.0).astype(obuf.dtype)

    out = pltpu.make_async_copy(obuf, own_out, o_sem)
    out.start()
    width = area.shape[1]
    rows = pool.shape[1]
    n9 = width // 4
    row = lax.broadcasted_iota(jnp.int32, (rows, width), 0)
    pixel = lax.broadcasted_iota(jnp.int32, (rows, width), 1)
    member = jnp.where(row < n9, pixel // 4 - row, pixel // 16 - (row - n9)) == 0

    @pl.loop(0, owned)
    def _(t):
        share = jnp.where(member, area[pl.ds(t, 1), :], 0.0)
        pool[t] = (share / share.sum(1, keepdims=True)).astype(pool.dtype)

    out.wait()
    for copy in moved:
        copy.wait()


def exchange(sends, table, fields, weights, source_block, area, sectors, groups_dev):
    nb, width, _ = weights.shape
    cols = fields.shape[-1]
    owned = area.shape[0]
    block = (width, cols)
    vmem = pl.BlockSpec(memory_space=pltpu.VMEM)
    kinds = len(MOVES)
    return pl.pallas_call(
        functools.partial(exchange_kernel, nb // groups_dev, sectors),
        out_shape=[jax.ShapeDtypeStruct((CAP, *block), jnp.bfloat16)] * kinds
        + [jax.ShapeDtypeStruct(table.shape, jnp.int32)] * kinds
        + [
            jax.ShapeDtypeStruct((owned, *block), jnp.bfloat16),
            jax.ShapeDtypeStruct((owned, width // 4 + width // 16, width), jnp.bfloat16),
        ],
        in_specs=[HBM] * (FIRST + 4) + [vmem],
        out_specs=[HBM] * (2 * kinds + 1) + [vmem],
        scratch_shapes=[
            pltpu.SMEM(table.shape, jnp.int32),
            pltpu.SMEM((nb,), jnp.int32),
            pltpu.VMEM(weights.shape, jnp.bfloat16),
            pltpu.VMEM(fields.shape, jnp.bfloat16),
            pltpu.VMEM((groups_dev, *block), jnp.bfloat16),
            pltpu.VMEM((owned, *block), jnp.bfloat16),
        ]
        + [
            pltpu.VMEM((CAP - (HEAD if k < FIRST else 0), *block), jnp.bfloat16)
            for k in range(kinds)
        ]
        + [
            pltpu.SemaphoreType.DMA((3 * kinds,)),
            pltpu.SemaphoreType.DMA((3 * kinds,)),
            pltpu.SemaphoreType.DMA((2,)),
            pltpu.SemaphoreType.DMA((groups_dev // CHUNK,)),
            pltpu.SemaphoreType.DMA((4,)),
            pltpu.SemaphoreType.DMA,
        ],
        compiler_params=pltpu.CompilerParams(
            collective_id=0, has_side_effects=True, vmem_limit_bytes=60 * 2**20
        ),
        name="exchange",
    )(*sends, table, source_block, weights, fields, area)


def combine_kernel(row, *refs):
    tables, received_hbm, own_hbm, pool_hbm = refs[:4], refs[4:8], refs[8], refs[9]
    outs_hbm = refs[10:13]
    slots, received, own, pool = refs[13:17], refs[17:21], refs[21], refs[22]
    outs, sem, own_sem, pool_sem, out_sem = refs[23:26], refs[26], refs[27], refs[28], refs[29]
    ten, nine, eight = outs
    chunks = own_sem.shape[0]
    step = own.shape[0] // chunks
    n9 = nine.shape[1]

    def part(source, place, c, semaphore):
        rows = pl.ds(c * step, step)
        return pltpu.make_async_copy(source.at[rows], place.at[rows], semaphore)

    def results(c):
        return [part(outs[i], outs_hbm[i], c, out_sem.at[3 * c + i]) for i in range(3)]

    copies = [
        pltpu.make_async_copy(table, slots[k], sem.at[k]) for k, table in enumerate(tables)
    ] + [
        pltpu.make_async_copy(block, received[k], sem.at[4 + k])
        for k, block in enumerate(received_hbm)
    ]
    for copy in copies:
        copy.start()
    for c in range(chunks):
        part(own_hbm, own, c, own_sem.at[c]).start()
        part(pool_hbm, pool, c, pool_sem.at[c]).start()
    for copy in copies:
        copy.wait()

    @pl.loop(0, chunks)
    def _(c):
        part(own_hbm, own, c, own_sem.at[c]).wait()
        part(pool_hbm, pool, c, pool_sem.at[c]).wait()
        for j in range(step):
            t = c * step + j
            total = own[t].astype(jnp.float32)
            for k in range(4):
                slot = slots[k][k * row + t]
                value = received[k][jnp.maximum(slot, 0)].astype(jnp.float32)
                total = total + jnp.where(slot >= 0, value, 0.0)
            rounded = total.astype(jnp.bfloat16)
            ten[t] = rounded
            means = jnp.dot(pool[t], rounded, preferred_element_type=jnp.float32)
            nine[t] = means[:n9]
            eight[t] = means[n9:]
        for copy in results(c):
            copy.start()

    @pl.loop(0, chunks)
    def _(c):
        for copy in results(c):
            copy.wait()


def combine(tables, own, received, pool):
    owned, width, cols = own.shape
    chunks = owned // STEP
    outs = [
        jax.ShapeDtypeStruct((owned, width, cols), jnp.bfloat16),
        jax.ShapeDtypeStruct((owned, width // 4, cols), jnp.float32),
        jax.ShapeDtypeStruct((owned, width // 16, cols), jnp.float32),
    ]
    return pl.pallas_call(
        functools.partial(combine_kernel, table_size(owned)[0]),
        out_shape=outs,
        in_specs=[HBM] * 10,
        out_specs=[HBM] * 3,
        scratch_shapes=[pltpu.SMEM(tables[0].shape, jnp.int32)] * 4
        + [pltpu.VMEM(received[0].shape, jnp.bfloat16)] * 4
        + [pltpu.VMEM(own.shape, jnp.bfloat16), pltpu.VMEM(pool.shape, jnp.bfloat16)]
        + [pltpu.VMEM(out.shape, out.dtype) for out in outs]
        + [
            pltpu.SemaphoreType.DMA((8,)),
            pltpu.SemaphoreType.DMA((chunks,)),
            pltpu.SemaphoreType.DMA((chunks,)),
            pltpu.SemaphoreType.DMA((3 * chunks,)),
        ],
        compiler_params=pltpu.CompilerParams(vmem_limit_bytes=60 * 2**20),
        name="combine",
    )(*tables, *received, own, pool)


def per_device(fields, weights, source_block, target_block, area):
    width = weights.shape[1]
    cols = fields.shape[1]
    owned = area.shape[0] // width
    sectors = lax.axis_size("sector")
    groups_dev = target_block.shape[0]
    blocks = fields.reshape(-1, width, cols)
    sent = outgoing(blocks, weights, source_block, target_block, owned, sectors)
    arrived = exchange(
        sent[:FIRST], sent[FIRST], blocks, weights, source_block, area.reshape(owned, width), sectors,
        groups_dev,
    )
    ten, nine, eight = combine(arrived[4:8], arrived[8], arrived[:4], arrived[9])
    return ten.reshape(-1, cols), nine.reshape(-1, cols), eight.reshape(-1, cols)


def solution(mesh):
    in_specs = (
        P(("groups", "sector"), None),
        P("sector", None, None),
        P("sector"),
        P("sector"),
        P("sector"),
    )
    out_specs = (P(("groups", "sector"), None),) * 3
    return jax.shard_map(
        per_device, mesh=mesh, in_specs=in_specs, out_specs=out_specs, check_vma=False
    )
```
